32 devices in a mesh: groups: 2 (over y), head: 8 (over z, x), blk: 2 (over core).
Axes of the slice: x: 2, y: 2, z: 4, core: 2. Of those that a mesh axis runs over, the one named last changes fastest.
Arguments:
- queries: bfloat16 [1024, 2048], P(('groups', 'head', 'blk')), parts along dimension 0, may hold values from -6 to 6
- key_rows: bfloat16 [1024, 256], P(('groups', 'head', 'blk')), parts along dimension 0, may hold values from -6 to 6
- value_rows: bfloat16 [1024, 256], P(('groups', 'head', 'blk')), parts along dimension 0, may hold values from -6 to 6
- fwd_output: bfloat16 [1024, 2048], P(('groups', 'head', 'blk')), parts along dimension 0, may hold values from -6 to 6
- grad_out: bfloat16 [1024, 2048], P(('groups', 'head', 'blk')), parts along dimension 0, may hold values from -6 to 6
- log_norm: float32 [1024, 16], P(('groups', 'head', 'blk')), parts along dimension 0, may hold values from 2 to 5.5
- visible: int32 [8, 4], P('groups'), parts along dimension 0, may hold values from 0 to 1, as said below
- seg_lengths: int32 [8], P('groups'), parts along dimension 0, may hold values from 1 to 256, 512 in all
Outputs:
- grad_queries: bfloat16 [1024, 2048], P(('groups', 'head', 'blk')), parts along dimension 0
- grad_keys: bfloat16 [1024, 256], P(('groups', 'head', 'blk')), parts along dimension 0
- grad_values: bfloat16 [1024, 256], P(('groups', 'head', 'blk')), parts along dimension 0
The draws below stay inside these ranges and needn't reach their ends.
There are 2 independent parts, one for each index of `groups`. The reference program is written for one: setup_inputs(seed, part) draws one part's arguments, and reference() takes and returns one part's arrays. A program takes and returns all parts, laid end to end along the dimension named above; each array names one. Nothing has to cross between parts.
Inputs may be any that keep to these rules, and one draw needn't show every extreme that they name: visible[a, b] is 1 exactly when block b is block a or an ancestor of block a in a tree over the 4 blocks whose root is block 0 and in which every block's parent comes before it.
All inputs are finite; a program needn't handle non-finite values.
Results may differ from the reference program's by a relative error of at most 0.0051.
Values may be sent and summed in bfloat16 or wider, within the bound.
A program may use at most 64 MiB of HBM per device.

```python
import math
import jax
import jax.numpy as jnp
import numpy as np
from jax import lax

DH = 128
QH = 16
KVH = 2
BLOCK = 128
NSEG = 4
SEQ = 512


def draw_visible(key, part):
    block_count = SEQ // BLOCK
    block_iota = jnp.arange(block_count, dtype=jnp.int32)
    tree_key = jax.random.fold_in(key, 7193)
    back_steps = jax.random.randint(tree_key, (block_count,), 0, 4, dtype=jnp.int32)
    parent = jnp.maximum(block_iota - 1 - back_steps, 0)
    anc_table = (block_iota[:, None] == block_iota[None, :]).astype(jnp.int32)

    def climb(turn_index, carry_state):
        table_now, cursor = carry_state
        table_now = jnp.maximum(table_now, (cursor[:, None] == block_iota[None, :]).astype(jnp.int32))
        return (table_now, parent[cursor])
    anc_table, cursor = lax.fori_loop(0, block_count, climb, (anc_table, parent))
    return anc_table


def block_levels(rng, dims, cuts, low, high):
    factor_of, own = 1.0, jax.random.fold_in(rng, 6)
    for dim, parts in cuts:
        heights = jnp.exp(jax.random.uniform(jax.random.fold_in(own, dim), (parts,), jnp.float32, low / len(cuts), high / len(cuts)))
        factor_of = factor_of * jnp.repeat(heights, dims[dim] // parts).reshape([-1 if axis == dim else 1 for axis in range(len(dims))])
    return factor_of


def split_up(count, total, bound, skew):
    loads = [(1 << 20) // math.isqrt(standing ** skew) + 1 for standing in range(2, count + 1)]
    surplus, holding = total - bound - (count - 1), [1] * (count - 1)
    while surplus > 0:
        candidates = [i for i in range(count - 1) if holding[i] < bound]
        whole, remaining = sum([loads[i] for i in candidates]), surplus
        for i in candidates:
            more = min(bound - holding[i], max(1, remaining * loads[i] // whole), surplus)
            holding[i] = holding[i] + more
            surplus = surplus - more
    return np.array([bound] + holding)


def ragged(key, count, total, limit, slope):
    if count == 2:
        one = jax.random.randint(key, (), max(1, total - limit), min(limit, total - 1) + 1)
        return jnp.stack([one, total - one])
    tallies = jnp.asarray(split_up(count, total, limit, slope), jnp.int32)
    couples = (count - 1) // 2
    giver, receiver = tallies[1:1 + 2 * couples:2], tallies[2:2 + 2 * couples:2]
    room = jnp.minimum(giver - 1, limit - receiver)
    passed = jax.random.randint(jax.random.fold_in(key, 1), (couples,), 0, 1 << 20) % (room + 1)
    tallies = tallies.at[1:1 + 2 * couples:2].set(giver - passed).at[2:2 + 2 * couples:2].set(receiver + passed)
    return tallies[jax.random.permutation(jax.random.fold_in(key, 2), count)]


def centred(own_key, dims, scale, limit, cuts=(), kind=jnp.bfloat16):
    loudness = block_levels(own_key, dims, cuts, -0.22, 0.18) if cuts else 1.0
    result = jax.random.normal(own_key, dims, jnp.float32) * scale * loudness
    return jnp.minimum(jnp.maximum(result, -limit), limit).astype(kind)


def setup_inputs(seed: int = 0, part: int = 0) -> dict:
    key_of = jax.random.split(jax.random.key(seed), 9)
    own_keys = jax.random.split(jax.random.fold_in(key_of[8], part), 9)
    queries = centred(own_keys[0], (SEQ, QH * DH), 1.0, 6.0, ((0, 16),))
    key_rows = centred(own_keys[1], (SEQ, KVH * DH), 1.0, 6.0, ((0, 16),))
    value_rows = centred(own_keys[2], (SEQ, KVH * DH), 1.0, 6.0, ((0, 16),))
    fwd_output = centred(own_keys[3], (SEQ, QH * DH), 1.0, 6.0, ((0, 16),))
    grad_out = centred(own_keys[4], (SEQ, QH * DH), 1.0, 6.0, ((0, 16),))
    log_norm = jnp.clip(2.0 + 3.5 * jax.random.uniform(own_keys[5], (SEQ, QH), jnp.float32) ** block_levels(own_keys[5], (SEQ, QH), ((0, 16),), -0.2, 0.2), 2.0, 5.5)
    visible = draw_visible(jax.random.fold_in(jax.random.fold_in(key_of[8], part), 71), part)
    seg_lengths = ragged(own_keys[7], NSEG, SEQ, SEQ // 2, 0).astype(jnp.int32)
    return {"queries": queries, "key_rows": key_rows, "value_rows": value_rows, "fwd_output": fwd_output, "grad_out": grad_out, "log_norm": log_norm, "visible": visible, "seg_lengths": seg_lengths}


def reference(queries, key_rows, value_rows, fwd_output, grad_out, log_norm, visible, seg_lengths):
    seq_len = queries.shape[0]
    group_size = QH // KVH
    softmax_scale = 1.0 / math.sqrt(DH)
    query_heads = queries.reshape(seq_len, QH, DH)
    grad_heads = grad_out.reshape(seq_len, QH, DH)
    out_heads = fwd_output.reshape(seq_len, QH, DH)
    row_delta = lax.optimization_barrier(jnp.sum(grad_heads.astype(jnp.float32) * out_heads.astype(jnp.float32), axis=2))
    key_heads = key_rows.reshape(seq_len, KVH, DH)
    value_heads = value_rows.reshape(seq_len, KVH, DH)
    positions = jnp.arange(seq_len, dtype=jnp.int32)
    seg_ends = jnp.cumsum(seg_lengths).astype(jnp.int32)
    seg_ids = lax.optimization_barrier(jnp.sum((positions[:, None] >= seg_ends[None, :]).astype(jnp.int32), axis=1))
    block_ids = positions // BLOCK
    tile_count = seq_len // BLOCK

    def one_head(head):
        kv_head = head // group_size
        query_h = query_heads[:, head, :]
        grad_h = grad_heads[:, head, :]
        key_h = key_heads[:, kv_head, :]
        value_h = value_heads[:, kv_head, :]
        lse_h = log_norm[:, head]
        delta_h = row_delta[:, head]

        def tile_step(carry_state, tile):
            key_sum, value_sum = carry_state
            start = (tile * BLOCK).astype(jnp.int32)
            query_tile = lax.dynamic_slice_in_dim(query_h, start, BLOCK, 0)
            grad_tile = lax.dynamic_slice_in_dim(grad_h, start, BLOCK, 0)
            lse_tile = lax.dynamic_slice_in_dim(lse_h, start, BLOCK, 0)
            delta_tile = lax.dynamic_slice_in_dim(delta_h, start, BLOCK, 0)
            tile_pos = start + jnp.arange(BLOCK, dtype=jnp.int32)
            tile_seg = lax.dynamic_slice_in_dim(seg_ids, start, BLOCK, 0)
            tile_block = tile_pos // BLOCK
            reach_table = visible[tile_block[:, None], block_ids[None, :]] > 0
            same_doc = tile_seg[:, None] == seg_ids[None, :]
            earlier = (tile_block[:, None] != block_ids[None, :]) | (positions[None, :] <= tile_pos[:, None])
            allowed = reach_table & same_doc & earlier
            scores = jnp.dot(query_tile, key_h.T, preferred_element_type=jnp.float32) * softmax_scale
            prob_full = jnp.where(allowed, jnp.exp(scores - lse_tile[:, None]), 0.0)
            prob_half = prob_full.astype(jnp.bfloat16)
            value_sum = value_sum + jnp.dot(prob_half.T, grad_tile, preferred_element_type=jnp.float32)
            grad_prob = jnp.dot(grad_tile, value_h.T, preferred_element_type=jnp.float32)
            grad_score = (prob_full * (grad_prob - delta_tile[:, None]) * softmax_scale).astype(jnp.bfloat16)
            query_tile_grad = jnp.dot(grad_score, key_h, preferred_element_type=jnp.float32)
            key_sum = key_sum + jnp.dot(grad_score.T, query_tile, preferred_element_type=jnp.float32)
            return ((key_sum, value_sum), query_tile_grad)
        zero_rows = jnp.zeros((seq_len, DH), jnp.float32)
        sums, query_tiles = lax.scan(tile_step, (zero_rows, zero_rows), jnp.arange(tile_count, dtype=jnp.int32))
        return (query_tiles.reshape(seq_len, DH), sums[0], sums[1])
    query_all, key_all, value_all = lax.map(one_head, jnp.arange(QH, dtype=jnp.int32))
    grad_queries = jnp.transpose(query_all, (1, 0, 2)).reshape(seq_len, QH * DH).astype(jnp.bfloat16)
    key_group = lax.optimization_barrier(jnp.sum(key_all.reshape(KVH, group_size, seq_len, DH), axis=1))
    value_group = lax.optimization_barrier(jnp.sum(value_all.reshape(KVH, group_size, seq_len, DH), axis=1))
    grad_keys = jnp.transpose(key_group, (1, 0, 2)).reshape(seq_len, KVH * DH).astype(jnp.bfloat16)
    grad_values = jnp.transpose(value_group, (1, 0, 2)).reshape(seq_len, KVH * DH).astype(jnp.bfloat16)
    return (grad_queries, grad_keys, grad_values)
```

```python
import functools
import math

import jax
import jax.numpy as jnp
from jax import lax
from jax.experimental import pallas as pl
from jax.experimental.pallas import tpu as pltpu
from jax.sharding import PartitionSpec as P

BLOCK = 128
CORES = 2
MESH = pl.DeviceIdType.MESH
NT = (((1,), (1,)), ((), ()))
TN = (((0,), (0,)), ((), ()))
NN = (((1,), (0,)), ((), ()))


def dot(a, b, dims):
    return lax.dot_general(a, b, dims, preferred_element_type=jnp.float32)


def each(first, last, body):
    if last - first <= 8:
        for k in range(first, last):
            body(k)
    else:
        lax.fori_loop(first, last, lambda k, c: (body(k), c)[1], 0)


def kernel(
    chips, reach, blk_size, group,
    vis_ref, seg_ref, q_hbm, k_hbm, v_hbm, o_hbm, g_hbm, l_hbm,
    dq_ref, dk_ref, dv_ref,
    q_in, k_in, v_in, o_in, g_in, l_in, in_sem,
    rows, rows_out, kv_out, kv, ds_all, part, back, own_part, dq_out, dq_back,
    x_send, x_recv, kv_send, kv_recv, part_send, part_recv, dq_send, dq_recv,
):
    tok, width = q_in.shape
    dh = k_in.shape[1] // CORES
    half = group * dh
    scale = 1.0 / math.sqrt(dh)
    spot = lax.axis_index("head") * blk_size + lax.axis_index("blk")
    chip, core = spot // CORES, spot % CORES
    other = 1 - core

    def at(its_chip, its_core):
        where = its_chip * CORES + its_core
        return {"head": where // blk_size, "blk": where % blk_size}

    def on_chips(first, last, sign, body):
        def one(k):
            its_chip = chip + sign * k

            @pl.when((its_chip >= 0) & (its_chip < chips))
            def _():
                body(k, its_chip)

        each(first, last, one)

    barrier = pltpu.get_barrier_semaphore()

    def greet(k, its_chip):
        for c in range(CORES):
            pl.semaphore_signal(barrier, inc=1, device_id=at(its_chip, c), device_id_type=MESH)

    loads = [
        pltpu.make_async_copy(src, dst, in_sem.at[i])
        for i, (src, dst) in enumerate(
            ((k_hbm, k_in), (v_hbm, v_in), (q_hbm, q_in), (g_hbm, g_in), (o_hbm, o_in), (l_hbm, l_in))
        )
    ]
    for load in loads:
        load.start()
    pl.semaphore_signal(barrier, inc=1, device_id=at(chip, other), device_id_type=MESH)
    on_chips(1, reach + 1, 1, greet)
    on_chips(1, reach + 1, -1, greet)

    loads[0].wait()
    loads[1].wait()
    for c in range(CORES):
        kv_out[c, 0] = k_in[:, c * dh : (c + 1) * dh]
        kv_out[c, 1] = v_in[:, c * dh : (c + 1) * dh]
    kv[0, pl.ds(core, 1)] = kv_out[pl.ds(core, 1)]

    near = jnp.minimum(chip, reach) + jnp.minimum(chips - 1 - chip, reach)
    pl.semaphore_wait(barrier, CORES * near + 1)

    def kv_copy(k, its_chip, its_core):
        return pltpu.make_async_remote_copy(
            src_ref=kv_out.at[its_core],
            dst_ref=kv.at[k, core],
            send_sem=kv_send.at[k, its_core],
            recv_sem=kv_recv.at[k, core],
            device_id=at(its_chip, its_core),
            device_id_type=MESH,
        )

    def kv_arrived(k, its_chip, its_core):
        pltpu.make_async_remote_copy(
            src_ref=kv_out.at[0],
            dst_ref=kv.at[k, its_core],
            send_sem=kv_send.at[k, its_core],
            recv_sem=kv_recv.at[k, its_core],
            device_id=at(its_chip, its_core),
            device_id_type=MESH,
        ).wait_recv()

    def send_kv(k, its_chip):
        for c in range(CORES):
            kv_copy(k, its_chip, c).start()

    on_chips(1, reach + 1, 1, send_kv)
    kv_copy(0, chip, other).start()

    for load in loads[2:]:
        load.wait()

    lane = lax.broadcasted_iota(jnp.int32, (tok, dh), 1)

    def prepare(h, column):
        at_h = pl.ds(pl.multiple_of(column * dh, dh), dh)
        g_h = g_in[:, at_h]
        delta = jnp.sum(g_h.astype(jnp.float32) * o_in[:, at_h].astype(jnp.float32), axis=1, keepdims=True)
        return at_h, g_h, delta

    def extra(lse, delta):
        value = jnp.where(lane < 3, lse * (1.0 / scale), jnp.where(lane < 6, delta, 0.0))
        high = value.astype(jnp.bfloat16).astype(jnp.float32)
        rest = value - high
        middle = rest.astype(jnp.bfloat16).astype(jnp.float32)
        third = (lane == 0) | (lane == 3)
        second = (lane == 1) | (lane == 4)
        return jnp.where(third, high, jnp.where(second, middle, rest - middle)).astype(jnp.bfloat16)

    def fill(target, mine):
        base = mine * group
        lse_all = jnp.where(mine == 0, l_in[:, :group], l_in[:, group:])
        for h in range(group):
            at_h, g_h, delta = prepare(h, base + h)
            r = slice(h * tok, (h + 1) * tok)
            target[0, r] = q_in[:, at_h]
            target[1, r] = extra(lse_all[:, h : h + 1], delta)
            target[2, r] = g_h

    fill(rows_out, other)
    x_copy = pltpu.make_async_remote_copy(
        src_ref=rows_out,
        dst_ref=rows.at[core],
        send_sem=x_send,
        recv_sem=x_recv,
        device_id=at(chip, other),
        device_id_type=MESH,
    )
    x_copy.start()
    fill(rows.at[core], core)

    n_rows = group * tok
    row_iota = lax.broadcasted_iota(jnp.int32, (1, n_rows), 1) % tok
    starts, spots = [], []
    for e in range(CORES):
        query_pos = (chip * CORES + e) * tok + row_iota
        start = jnp.zeros_like(query_pos)
        end = jnp.int32(0)
        for s in range(seg_ref.shape[0]):
            end = end + seg_ref[s]
            start = jnp.where(query_pos >= end, end, start)
        starts.append(start)
        spots.append(query_pos)
    chunk = CORES * tok
    chunk_lane = lax.broadcasted_iota(jnp.int32, (chunk, dh), 1)
    minus_lse = jnp.where(chunk_lane < 3, -1.0, 0.0).astype(jnp.bfloat16)
    minus_delta = jnp.where((chunk_lane >= 3) & (chunk_lane < 6), -1.0, 0.0).astype(jnp.bfloat16)
    key_iota = lax.broadcasted_iota(jnp.int32, (chunk, n_rows), 0)
    my_block = chip * chunk // BLOCK
    far = chips * chunk

    def grads(k, its_chip, diagonal):
        keys = jnp.concatenate([kv[k, 0, 0], kv[k, 1, 0]], axis=0)
        values = jnp.concatenate([kv[k, 0, 1], kv[k, 1, 1]], axis=0)
        keys_more = jnp.concatenate([keys, minus_lse], axis=1)
        values_more = jnp.concatenate([values, minus_delta], axis=1)
        seen = vis_ref[my_block, its_chip * chunk // BLOCK]
        key_pos = key_iota + its_chip * chunk
        key_grad = value_grad = None
        for e in range(CORES):
            q, more, g = rows[e, 0], rows[e, 1], rows[e, 2]
            scores = dot(keys_more, jnp.concatenate([q, more], axis=1), NT)
            grad_prob = dot(values_more, jnp.concatenate([g, more], axis=1), NT)
            allowed = key_pos >= jnp.where(seen > 0, starts[e], far)
            if diagonal:
                allowed = allowed & (key_pos <= spots[e])
            prob = jnp.where(allowed, jnp.exp(scores * scale), 0.0)
            grad_score = (prob * grad_prob * scale).astype(jnp.bfloat16)
            v_part = dot(prob.astype(jnp.bfloat16), g, NN)
            k_part = dot(grad_score, q, NN)
            ds_all[k, :, e * n_rows : (e + 1) * n_rows] = grad_score
            key_grad = k_part if key_grad is None else key_grad + k_part
            value_grad = v_part if value_grad is None else value_grad + v_part
        for e in range(CORES):
            part[k, e, 0] = key_grad[e * tok : (e + 1) * tok].astype(jnp.bfloat16)
            part[k, e, 1] = value_grad[e * tok : (e + 1) * tok].astype(jnp.bfloat16)
        return key_grad, value_grad

    def part_copy(k, its_chip, its_core):
        return pltpu.make_async_remote_copy(
            src_ref=part.at[k, its_core],
            dst_ref=back.at[k, core],
            send_sem=part_send.at[k, its_core],
            recv_sem=part_recv.at[k, core],
            device_id=at(its_chip, its_core),
            device_id_type=MESH,
        )

    def part_arrived(k, its_chip, its_core):
        pltpu.make_async_remote_copy(
            src_ref=part.at[k, its_core],
            dst_ref=back.at[k, its_core],
            send_sem=part_send.at[k, its_core],
            recv_sem=part_recv.at[k, its_core],
            device_id=at(its_chip, its_core),
            device_id_type=MESH,
        ).wait_recv()

    kv_arrived(0, chip, other)
    x_copy.wait_recv()
    grads(0, chip, True)
    part_copy(0, chip, other).start()
    back[0, pl.ds(core, 1)] = part[0, pl.ds(core, 1)]

    def one_chunk(k):
        its_chip = chip - k

        @pl.when(its_chip >= 0)
        def _():
            for e in range(CORES):
                kv_arrived(k, its_chip, e)
            grads(k, its_chip, False)
            for e in range(CORES):
                part_copy(k, its_chip, e).start()

        @pl.when(its_chip < 0)
        def _():
            kv[k] = jnp.zeros(kv.shape[1:], kv.dtype)
            ds_all[k] = jnp.zeros(ds_all.shape[1:], ds_all.dtype)

    each(1, reach + 1, one_chunk)

    total = reach + 1
    at_once = max(n for n in range(1, 9) if total % n == 0)

    def query_part(first):
        scores = jnp.concatenate([ds_all[first + i] for i in range(at_once)], axis=0)
        keys = jnp.concatenate(
            [kv[first + i, e, 0] for i in range(at_once) for e in range(CORES)], axis=0
        )
        return dot(scores, keys, TN)

    if total == at_once:
        query_grad = query_part(0)
    else:
        query_grad = lax.fori_loop(
            0, total // at_once, lambda i, acc: acc + query_part(i * at_once),
            jnp.zeros((CORES * n_rows, dh), jnp.float32),
        )
    for e in range(CORES):
        dq_out[e] = query_grad[e * n_rows : (e + 1) * n_rows].astype(jnp.bfloat16)
    dq_copy = pltpu.make_async_remote_copy(
        src_ref=dq_out.at[other],
        dst_ref=dq_back,
        send_sem=dq_send,
        recv_sem=dq_recv,
        device_id=at(chip, other),
        device_id_type=MESH,
    )
    dq_copy.start()
    for h in range(group):
        r = slice(h * tok, (h + 1) * tok)
        dq_ref[:, pl.ds(pl.multiple_of((core * group + h) * dh, dh), dh)] = dq_out[core, r]
    dq_copy.wait_recv()
    for h in range(group):
        r = slice(h * tok, (h + 1) * tok)
        dq_ref[:, pl.ds(pl.multiple_of((other * group + h) * dh, dh), dh)] = dq_back[r]

    part_arrived(0, chip, other)
    for c in range(CORES):
        for which in range(2):
            own_part[c, which] = back[0, c, which].astype(jnp.float32)

    def add(k, its_chip):
        for c in range(CORES):
            part_arrived(k, its_chip, c)
            own_part[c] += back[k, c].astype(jnp.float32)

    on_chips(1, reach + 1, 1, add)
    for c in range(CORES):
        dk_ref[:, c * dh : (c + 1) * dh] = own_part[c, 0].astype(jnp.bfloat16)
        dv_ref[:, c * dh : (c + 1) * dh] = own_part[c, 1].astype(jnp.bfloat16)

    x_copy.wait_send()
    dq_copy.wait_send()
    kv_copy(0, chip, other).wait_send()
    part_copy(0, chip, other).wait_send()

    def kv_left(k, its_chip):
        for c in range(CORES):
            kv_copy(k, its_chip, c).wait_send()

    def part_left(k, its_chip):
        for c in range(CORES):
            part_copy(k, its_chip, c).wait_send()

    on_chips(1, reach + 1, 1, kv_left)
    on_chips(1, reach + 1, -1, part_left)


def solution(mesh):
    blk_size = mesh.shape["blk"]
    devices = mesh.shape["head"] * blk_size
    chips = devices // CORES

    def shards(queries, key_rows, value_rows, fwd_output, grad_out, log_norm, visible, seg_lengths):
        tok, width = queries.shape
        heads = log_norm.shape[1]
        dh = width // heads
        kv_heads = key_rows.shape[1] // dh
        assert kv_heads == CORES and blk_size % CORES == 0 and BLOCK % (CORES * tok) == 0
        group = heads // kv_heads
        longest = devices * tok // 2
        reach = min(pl.cdiv(longest - 1, CORES * tok), chips - 1)
        n_rows = group * tok
        bf16, f32 = jnp.bfloat16, jnp.float32
        slots = reach + 1
        dma = pltpu.SemaphoreType.DMA
        return pl.pallas_call(
            functools.partial(kernel, chips, reach, blk_size, group),
            out_shape=(
                jax.ShapeDtypeStruct(queries.shape, bf16),
                jax.ShapeDtypeStruct(key_rows.shape, bf16),
                jax.ShapeDtypeStruct(value_rows.shape, bf16),
            ),
            in_specs=[pl.BlockSpec(memory_space=pltpu.SMEM)] * 2
            + [pl.BlockSpec(memory_space=pl.ANY)] * 6,
            out_specs=[pl.BlockSpec(memory_space=pltpu.VMEM)] * 3,
            scratch_shapes=[
                pltpu.VMEM(queries.shape, bf16),
                pltpu.VMEM(key_rows.shape, bf16),
                pltpu.VMEM(value_rows.shape, bf16),
                pltpu.VMEM(fwd_output.shape, bf16),
                pltpu.VMEM(grad_out.shape, bf16),
                pltpu.VMEM(log_norm.shape, f32),
                dma((6,)),
                pltpu.VMEM((CORES, 3, n_rows, dh), bf16),
                pltpu.VMEM((3, n_rows, dh), bf16),
                pltpu.VMEM((CORES, 2, tok, dh), bf16),
                pltpu.VMEM((slots, CORES, 2, tok, dh), bf16),
                pltpu.VMEM((slots, CORES * tok, CORES * n_rows), bf16),
                pltpu.VMEM((slots, CORES, 2, tok, dh), bf16),
                pltpu.VMEM((slots, CORES, 2, tok, dh), bf16),
                pltpu.VMEM((CORES, 2, tok, dh), f32),
                pltpu.VMEM((CORES, n_rows, dh), bf16),
                pltpu.VMEM((n_rows, dh), bf16),
                dma, dma,
                dma((slots, CORES)), dma((slots, CORES)),
                dma((slots, CORES)), dma((slots, CORES)),
                dma, dma,
            ],
            compiler_params=pltpu.CompilerParams(
                collective_id=0, has_side_effects=True, vmem_limit_bytes=48 << 20
            ),
        )(visible, seg_lengths, queries, key_rows, value_rows, fwd_output, grad_out, log_norm)

    tokens = P(("groups", "head", "blk"), None)
    return jax.shard_map(
        shards,
        mesh=mesh,
        in_specs=(tokens,) * 6 + (P("groups", None), P("groups")),
        out_specs=(tokens,) * 3,
        check_vma=False,
    )
```

```python
import functools
import math

import jax
import jax.numpy as jnp
from jax import lax
from jax.experimental import pallas as pl
from jax.experimental.pallas import tpu as pltpu
from jax.sharding import PartitionSpec as P

BLOCK = 128
CORES = 2
MESH = pl.DeviceIdType.MESH
NT = (((1,), (1,)), ((), ()))
TN = (((0,), (0,)), ((), ()))
NN = (((1,), (0,)), ((), ()))


def dot(a, b, dims):
    return lax.dot_general(a, b, dims, preferred_element_type=jnp.float32)


def each(first, last, body):
    if last - first <= 8:
        for k in range(first, last):
            body(k)
    else:
        lax.fori_loop(first, last, lambda k, c: (body(k), c)[1], 0)


def kernel(
    chips, reach, blk_size, group,
    vis_ref, seg_ref, q_hbm, k_hbm, v_hbm, o_hbm, g_hbm, l_hbm,
    dq_hbm, dk_hbm, dv_hbm,
    dq_ref, dk_ref, dv_ref, out_sem,
    q_in, k_in, v_in, o_in, g_in, l_in, in_sem,
    rows, rows_out, kv_out, kv, ds_all, part, back, own_part, dq_out, dq_back,
    x_send, x_recv, kv_send, kv_recv, part_send, part_recv, dq_send, dq_recv,
):
    tok, width = q_in.shape
    dh = k_in.shape[1] // CORES
    half = group * dh
    scale = 1.0 / math.sqrt(dh)
    spot = lax.axis_index("head") * blk_size + lax.axis_index("blk")
    chip, core = spot // CORES, spot % CORES
    other = 1 - core

    def at(its_chip, its_core):
        where = its_chip * CORES + its_core
        return {"head": where // blk_size, "blk": where % blk_size}

    def on_chips(first, last, sign, body):
        def one(k):
            its_chip = chip + sign * k

            @pl.when((its_chip >= 0) & (its_chip < chips))
            def _():
                body(k, its_chip)

        each(first, last, one)

    barrier = pltpu.get_barrier_semaphore()

    def greet(k, its_chip):
        for c in range(CORES):
            pl.semaphore_signal(barrier, inc=1, device_id=at(its_chip, c), device_id_type=MESH)

    loads = [
        pltpu.make_async_copy(src, dst, in_sem.at[i])
        for i, (src, dst) in enumerate(
            ((k_hbm, k_in), (v_hbm, v_in), (q_hbm, q_in), (g_hbm, g_in), (o_hbm, o_in), (l_hbm, l_in))
        )
    ]
    for load in loads:
        load.start()
    pl.semaphore_signal(barrier, inc=1, device_id=at(chip, other), device_id_type=MESH)
    on_chips(1, reach + 1, 1, greet)
    on_chips(1, reach + 1, -1, greet)

    for load in loads:
        load.wait()
    for c in range(CORES):
        kv_out[c, 0] = k_in[:, c * dh : (c + 1) * dh]
        kv_out[c, 1] = v_in[:, c * dh : (c + 1) * dh]
    kv[0, pl.ds(core, 1)] = kv_out[pl.ds(core, 1)]

    lane = lax.broadcasted_iota(jnp.int32, (tok, dh), 1)

    lse_in = jnp.transpose(l_in[...])

    def prepare(column):
        at_h = pl.ds(pl.multiple_of(column * dh, dh), dh)
        g_h = g_in[:, at_h]
        delta = jnp.sum(g_h.astype(jnp.float32) * o_in[:, at_h].astype(jnp.float32), axis=1, keepdims=True)
        return at_h, g_h, delta

    def extra(lse, delta):
        value = jnp.where(lane < 3, lse * (1.0 / scale), jnp.where(lane < 6, delta, 0.0))
        high = value.astype(jnp.bfloat16).astype(jnp.float32)
        rest = value - high
        middle = rest.astype(jnp.bfloat16).astype(jnp.float32)
        third = (lane == 0) | (lane == 3)
        second = (lane == 1) | (lane == 4)
        return jnp.where(third, high, jnp.where(second, middle, rest - middle)).astype(jnp.bfloat16)

    def fill(target, mine):
        base = mine * group
        lse_all = jnp.where(mine == 0, lse_in[:, :group], lse_in[:, group:])
        for h in range(group):
            at_h, g_h, delta = prepare(base + h)
            r = slice(h * tok, (h + 1) * tok)
            target[0, r] = q_in[:, at_h]
            target[1, r] = extra(lse_all[:, h : h + 1], delta)
            target[2, r] = g_h

    fill(rows_out, other)

    near = jnp.minimum(chip, reach) + jnp.minimum(chips - 1 - chip, reach)
    pl.semaphore_wait(barrier, CORES * near + 1)

    def kv_copy(k, its_chip, its_core):
        return pltpu.make_async_remote_copy(
            src_ref=kv_out.at[its_core],
            dst_ref=kv.at[k, core],
            send_sem=kv_send.at[k, its_core],
            recv_sem=kv_recv.at[k, core],
            device_id=at(its_chip, its_core),
            device_id_type=MESH,
        )

    def kv_arrived(k, its_chip, its_core):
        pltpu.make_async_remote_copy(
            src_ref=kv_out.at[0],
            dst_ref=kv.at[k, its_core],
            send_sem=kv_send.at[k, its_core],
            recv_sem=kv_recv.at[k, its_core],
            device_id=at(its_chip, its_core),
            device_id_type=MESH,
        ).wait_recv()

    def send_kv(k, its_chip):
        for c in range(CORES):
            kv_copy(k, its_chip, c).start()

    on_chips(1, reach + 1, 1, send_kv)
    kv_copy(0, chip, other).start()

    x_copy = pltpu.make_async_remote_copy(
        src_ref=rows_out,
        dst_ref=rows.at[core],
        send_sem=x_send,
        recv_sem=x_recv,
        device_id=at(chip, other),
        device_id_type=MESH,
    )
    x_copy.start()
    fill(rows.at[core], core)

    n_rows = group * tok
    row_iota = lax.broadcasted_iota(jnp.int32, (1, n_rows), 1) % tok
    starts, spots = [], []
    for e in range(CORES):
        query_pos = (chip * CORES + e) * tok + row_iota
        start = jnp.zeros_like(query_pos)
        end = jnp.int32(0)
        for s in range(seg_ref.shape[0]):
            end = end + seg_ref[s]
            start = jnp.where(query_pos >= end, end, start)
        starts.append(start)
        spots.append(query_pos)
    chunk = CORES * tok
    chunk_lane = lax.broadcasted_iota(jnp.int32, (chunk, dh), 1)
    minus_lse = jnp.where(chunk_lane < 3, -1.0, 0.0).astype(jnp.bfloat16)
    minus_delta = jnp.where((chunk_lane >= 3) & (chunk_lane < 6), -1.0, 0.0).astype(jnp.bfloat16)
    key_iota = lax.broadcasted_iota(jnp.int32, (chunk, n_rows), 0)
    my_block = chip * chunk // BLOCK
    far = chips * chunk

    def grads(k, its_chip, diagonal):
        keys = jnp.concatenate([kv[k, 0, 0], kv[k, 1, 0]], axis=0)
        values = jnp.concatenate([kv[k, 0, 1], kv[k, 1, 1]], axis=0)
        keys_more = jnp.concatenate([keys, minus_lse], axis=1)
        values_more = jnp.concatenate([values, minus_delta], axis=1)
        seen = vis_ref[my_block, its_chip * chunk // BLOCK]
        key_pos = key_iota + its_chip * chunk
        key_grad = value_grad = None
        for e in range(CORES):
            q, more, g = rows[e, 0], rows[e, 1], rows[e, 2]
            scores = dot(keys_more, jnp.concatenate([q, more], axis=1), NT)
            grad_prob = dot(values_more, jnp.concatenate([g, more], axis=1), NT)
            allowed = key_pos >= jnp.where(seen > 0, starts[e], far)
            if diagonal:
                allowed = allowed & (key_pos <= spots[e])
            prob = jnp.where(allowed, jnp.exp(scores * scale), 0.0)
            grad_score = (prob * grad_prob * scale).astype(jnp.bfloat16)
            v_part = dot(prob.astype(jnp.bfloat16), g, NN)
            k_part = dot(grad_score, q, NN)
            ds_all[k, :, e * n_rows : (e + 1) * n_rows] = grad_score
            key_grad = k_part if key_grad is None else key_grad + k_part
            value_grad = v_part if value_grad is None else value_grad + v_part
        for e in range(CORES):
            part[k, e, 0] = key_grad[e * tok : (e + 1) * tok].astype(jnp.bfloat16)
            part[k, e, 1] = value_grad[e * tok : (e + 1) * tok].astype(jnp.bfloat16)
        return key_grad, value_grad

    def part_copy(k, its_chip, its_core):
        return pltpu.make_async_remote_copy(
            src_ref=part.at[k, its_core],
            dst_ref=back.at[k, core],
            send_sem=part_send.at[k, its_core],
            recv_sem=part_recv.at[k, core],
            device_id=at(its_chip, its_core),
            device_id_type=MESH,
        )

    def part_arrived(k, its_chip, its_core):
        pltpu.make_async_remote_copy(
            src_ref=part.at[k, its_core],
            dst_ref=back.at[k, its_core],
            send_sem=part_send.at[k, its_core],
            recv_sem=part_recv.at[k, its_core],
            device_id=at(its_chip, its_core),
            device_id_type=MESH,
        ).wait_recv()

    kv_arrived(0, chip, other)
    x_copy.wait_recv()
    grads(0, chip, True)
    part_copy(0, chip, other).start()
    back[0, pl.ds(core, 1)] = part[0, pl.ds(core, 1)]

    def one_chunk(k):
        its_chip = chip - k

        @pl.when(its_chip >= 0)
        def _():
            for e in range(CORES):
                kv_arrived(k, its_chip, e)
            grads(k, its_chip, False)
            for e in range(CORES):
                part_copy(k, its_chip, e).start()

        @pl.when(its_chip < 0)
        def _():
            kv[k] = jnp.zeros(kv.shape[1:], kv.dtype)
            ds_all[k] = jnp.zeros(ds_all.shape[1:], ds_all.dtype)

    each(1, reach + 1, one_chunk)

    total = reach + 1
    at_once = max(n for n in range(1, 9) if total % n == 0)

    def query_part(first):
        scores = jnp.concatenate([ds_all[first + i] for i in range(at_once)], axis=0)
        keys = jnp.concatenate(
            [kv[first + i, e, 0] for i in range(at_once) for e in range(CORES)], axis=0
        )
        return dot(scores, keys, TN)

    if total == at_once:
        query_grad = query_part(0)
    else:
        query_grad = lax.fori_loop(
            0, total // at_once, lambda i, acc: acc + query_part(i * at_once),
            jnp.zeros((CORES * n_rows, dh), jnp.float32),
        )
    for e in range(CORES):
        dq_out[e] = query_grad[e * n_rows : (e + 1) * n_rows].astype(jnp.bfloat16)
    dq_copy = pltpu.make_async_remote_copy(
        src_ref=dq_out.at[other],
        dst_ref=dq_back,
        send_sem=dq_send,
        recv_sem=dq_recv,
        device_id=at(chip, other),
        device_id_type=MESH,
    )
    dq_copy.start()
    for h in range(group):
        r = slice(h * tok, (h + 1) * tok)
        dq_ref[:, pl.ds(pl.multiple_of((core * group + h) * dh, dh), dh)] = dq_out[core, r]
    dq_copy.wait_recv()
    for h in range(group):
        r = slice(h * tok, (h + 1) * tok)
        dq_ref[:, pl.ds(pl.multiple_of((other * group + h) * dh, dh), dh)] = dq_back[r]

    stores = [
        pltpu.make_async_copy(src, dst, out_sem.at[i])
        for i, (src, dst) in enumerate(((dq_ref, dq_hbm), (dk_ref, dk_hbm), (dv_ref, dv_hbm)))
    ]
    stores[0].start()

    part_arrived(0, chip, other)
    for c in range(CORES):
        for which in range(2):
            own_part[c, which] = back[0, c, which].astype(jnp.float32)

    def add(k, its_chip):
        for c in range(CORES):
            part_arrived(k, its_chip, c)
            own_part[c] += back[k, c].astype(jnp.float32)

    on_chips(1, reach + 1, 1, add)
    for c in range(CORES):
        dk_ref[:, c * dh : (c + 1) * dh] = own_part[c, 0].astype(jnp.bfloat16)
        dv_ref[:, c * dh : (c + 1) * dh] = own_part[c, 1].astype(jnp.bfloat16)
    stores[1].start()
    stores[2].start()

    x_copy.wait_send()
    dq_copy.wait_send()
    kv_copy(0, chip, other).wait_send()
    part_copy(0, chip, other).wait_send()

    def kv_left(k, its_chip):
        for c in range(CORES):
            kv_copy(k, its_chip, c).wait_send()

    def part_left(k, its_chip):
        for c in range(CORES):
            part_copy(k, its_chip, c).wait_send()

    on_chips(1, reach + 1, 1, kv_left)
    on_chips(1, reach + 1, -1, part_left)
    for copy in stores:
        copy.wait()


def store(a_in, b_in, c_in, a_out, b_out, c_out, sem):
    copies = [
        pltpu.make_async_copy(src, dst, sem.at[i])
        for i, (src, dst) in enumerate(((a_in, a_out), (b_in, b_out), (c_in, c_out)))
    ]
    for copy in copies:
        copy.start()
    for copy in copies:
        copy.wait()


def solution(mesh):
    blk_size = mesh.shape["blk"]
    devices = mesh.shape["head"] * blk_size
    chips = devices // CORES

    def shards(queries, key_rows, value_rows, fwd_output, grad_out, log_norm, visible, seg_lengths):
        tok, width = queries.shape
        heads = log_norm.shape[1]
        dh = width // heads
        kv_heads = key_rows.shape[1] // dh
        assert kv_heads == CORES and blk_size % CORES == 0 and BLOCK % (CORES * tok) == 0
        group = heads // kv_heads
        longest = devices * tok // 2
        reach = min(pl.cdiv(longest - 1, CORES * tok), chips - 1)
        n_rows = group * tok
        bf16, f32 = jnp.bfloat16, jnp.float32
        slots = reach + 1
        dma = pltpu.SemaphoreType.DMA
        grads = pl.pallas_call(
            functools.partial(kernel, chips, reach, blk_size, group),
            out_shape=(
                jax.ShapeDtypeStruct(queries.shape, bf16),
                jax.ShapeDtypeStruct(key_rows.shape, bf16),
                jax.ShapeDtypeStruct(value_rows.shape, bf16),
            ),
            in_specs=[pl.BlockSpec(memory_space=pltpu.SMEM)] * 2
            + [pl.BlockSpec(memory_space=pltpu.HBM)] * 6,
            out_specs=[pl.BlockSpec(memory_space=pltpu.HBM)] * 3,
            scratch_shapes=[
                pltpu.VMEM(queries.shape, bf16),
                pltpu.VMEM(key_rows.shape, bf16),
                pltpu.VMEM(value_rows.shape, bf16),
                dma((3,)),
                pltpu.VMEM(queries.shape, bf16),
                pltpu.VMEM(key_rows.shape, bf16),
                pltpu.VMEM(value_rows.shape, bf16),
                pltpu.VMEM(fwd_output.shape, bf16),
                pltpu.VMEM(grad_out.shape, bf16),
                pltpu.VMEM(log_norm.shape[::-1], f32),
                dma((6,)),
                pltpu.VMEM((CORES, 3, n_rows, dh), bf16),
                pltpu.VMEM((3, n_rows, dh), bf16),
                pltpu.VMEM((CORES, 2, tok, dh), bf16),
                pltpu.VMEM((slots, CORES, 2, tok, dh), bf16),
                pltpu.VMEM((slots, CORES * tok, CORES * n_rows), bf16),
                pltpu.VMEM((slots, CORES, 2, tok, dh), bf16),
                pltpu.VMEM((slots, CORES, 2, tok, dh), bf16),
                pltpu.VMEM((CORES, 2, tok, dh), f32),
                pltpu.VMEM((CORES, n_rows, dh), bf16),
                pltpu.VMEM((n_rows, dh), bf16),
                dma, dma,
                dma((slots, CORES)), dma((slots, CORES)),
                dma((slots, CORES)), dma((slots, CORES)),
                dma, dma,
            ],
            compiler_params=pltpu.CompilerParams(
                collective_id=0, has_side_effects=True, vmem_limit_bytes=56 << 20
            ),
        )(visible, seg_lengths, queries, key_rows, value_rows, fwd_output, grad_out, log_norm.T)

        return pl.pallas_call(
            store,
            out_shape=[jax.ShapeDtypeStruct(g.shape, g.dtype) for g in grads],
            in_specs=[pl.BlockSpec(memory_space=pltpu.HBM)] * 3,
            out_specs=[pl.BlockSpec(memory_space=pltpu.HBM)] * 3,
            scratch_shapes=[dma((3,))],
        )(*grads)

    tokens = P(("groups", "head", "blk"), None)
    return jax.shard_map(
        shards,
        mesh=mesh,
        in_specs=(tokens,) * 6 + (P("groups", None), P("groups")),
        out_specs=(tokens,) * 3,
        check_vma=False,
    )
```

```python
import functools
import math

import jax
import jax.numpy as jnp
from jax import lax
from jax.experimental import pallas as pl
from jax.experimental.pallas import tpu as pltpu
from jax.sharding import PartitionSpec as P

BLOCK = 128
CORES = 2
MESH = pl.DeviceIdType.MESH
NT = (((1,), (1,)), ((), ()))
TN = (((0,), (0,)), ((), ()))
NN = (((1,), (0,)), ((), ()))


def dot(a, b, dims):
    return lax.dot_general(a, b, dims, preferred_element_type=jnp.float32)


def each(first, last, body, down=False):
    if last - first <= 8:
        for k in range(last - 1, first - 1, -1) if down else range(first, last):
            body(k)
    else:
        lax.fori_loop(first, last, lambda k, c: (body(k), c)[1], 0)


def kernel(
    chips, reach, blk_size, group,
    vis_hbm, seg_hbm, q_hbm, k_hbm, v_hbm, o_hbm, g_hbm, l_hbm,
    dq_ref, dk_ref, dv_ref,
    vis_ref, seg_ref, q_in, k_in, v_in, o_in, g_in, l_in, in_sem,
    rows, rows_out, kv_out, kv, ds_all, part, back, own_part, dq_out, dq_back,
    x_send, x_recv, kv_send, kv_recv, part_send, part_recv, dq_send, dq_recv,
):
    tok, width = q_in.shape
    dh = k_in.shape[1] // CORES
    half = group * dh
    scale = 1.0 / math.sqrt(dh)
    spot = lax.axis_index("head") * blk_size + lax.axis_index("blk")
    chip, core = spot // CORES, spot % CORES
    other = 1 - core

    def at(its_chip, its_core):
        where = its_chip * CORES + its_core
        return {"head": where // blk_size, "blk": where % blk_size}

    def on_chips(first, last, sign, body, down=False):
        def one(k):
            its_chip = chip + sign * k

            @pl.when((its_chip >= 0) & (its_chip < chips))
            def _():
                body(k, its_chip)

        each(first, last, one, down)

    barrier = pltpu.get_barrier_semaphore()

    def greet(k, its_chip):
        for c in range(CORES):
            pl.semaphore_signal(barrier, inc=1, device_id=at(its_chip, c), device_id_type=MESH)

    loads = [
        pltpu.make_async_copy(src, dst, in_sem.at[i])
        for i, (src, dst) in enumerate(
            ((k_hbm, k_in), (v_hbm, v_in), (q_hbm, q_in), (g_hbm, g_in), (o_hbm, o_in), (l_hbm, l_in),
             (vis_hbm, vis_ref), (seg_hbm, seg_ref))
        )
    ]
    for load in loads:
        load.start()
    pl.semaphore_signal(barrier, inc=1, device_id=at(chip, other), device_id_type=MESH)
    on_chips(1, reach + 1, 1, greet)
    on_chips(1, reach + 1, -1, greet)

    for load in loads:
        load.wait()
    for c in range(CORES):
        kv_out[c, 0] = k_in[:, c * dh : (c + 1) * dh]
        kv_out[c, 1] = v_in[:, c * dh : (c + 1) * dh]
    kv[0, pl.ds(core, 1)] = kv_out[pl.ds(core, 1)]

    lane = lax.broadcasted_iota(jnp.int32, (tok, dh), 1)

    lse_in = jnp.transpose(l_in[...])

    def prepare(column):
        at_h = pl.ds(pl.multiple_of(column * dh, dh), dh)
        g_h = g_in[:, at_h]
        delta = jnp.sum(g_h.astype(jnp.float32) * o_in[:, at_h].astype(jnp.float32), axis=1, keepdims=True)
        return at_h, g_h, delta

    def extra(lse, delta):
        value = jnp.where(lane < 3, lse * (1.0 / scale), jnp.where(lane < 6, delta, 0.0))
        high = value.astype(jnp.bfloat16).astype(jnp.float32)
        rest = value - high
        middle = rest.astype(jnp.bfloat16).astype(jnp.float32)
        third = (lane == 0) | (lane == 3)
        second = (lane == 1) | (lane == 4)
        return jnp.where(third, high, jnp.where(second, middle, rest - middle)).astype(jnp.bfloat16)

    def fill(target, mine):
        base = mine * group
        lse_all = jnp.where(mine == 0, lse_in[:, :group], lse_in[:, group:])
        for h in range(group):
            at_h, g_h, delta = prepare(base + h)
            r = slice(h * tok, (h + 1) * tok)
            target[0, r] = q_in[:, at_h]
            target[1, r] = extra(lse_all[:, h : h + 1], delta)
            target[2, r] = g_h

    fill(rows_out, other)

    near = jnp.minimum(chip, reach) + jnp.minimum(chips - 1 - chip, reach)
    pl.semaphore_wait(barrier, CORES * near + 1)

    def kv_copy(k, its_chip, its_core):
        return pltpu.make_async_remote_copy(
            src_ref=kv_out.at[its_core],
            dst_ref=kv.at[k, core],
            send_sem=kv_send.at[k, its_core],
            recv_sem=kv_recv.at[k, core],
            device_id=at(its_chip, its_core),
            device_id_type=MESH,
        )

    def kv_arrived(k, its_chip, its_core):
        pltpu.make_async_remote_copy(
            src_ref=kv_out.at[0],
            dst_ref=kv.at[k, its_core],
            send_sem=kv_send.at[k, its_core],
            recv_sem=kv_recv.at[k, its_core],
            device_id=at(its_chip, its_core),
            device_id_type=MESH,
        ).wait_recv()

    def send_kv(k, its_chip):
        for c in range(CORES):
            kv_copy(k, its_chip, c).start()

    on_chips(1, reach + 1, 1, send_kv, True)
    kv_copy(0, chip, other).start()

    x_copy = pltpu.make_async_remote_copy(
        src_ref=rows_out,
        dst_ref=rows.at[core],
        send_sem=x_send,
        recv_sem=x_recv,
        device_id=at(chip, other),
        device_id_type=MESH,
    )
    x_copy.start()
    fill(rows.at[core], core)

    n_rows = group * tok
    row_iota = lax.broadcasted_iota(jnp.int32, (1, n_rows), 1) % tok
    starts, spots = [], []
    for e in range(CORES):
        query_pos = (chip * CORES + e) * tok + row_iota
        start = jnp.zeros_like(query_pos)
        end = jnp.int32(0)
        for s in range(seg_ref.shape[0]):
            end = end + seg_ref[s]
            start = jnp.where(query_pos >= end, end, start)
        starts.append(start)
        spots.append(query_pos)
    chunk = CORES * tok
    chunk_lane = lax.broadcasted_iota(jnp.int32, (chunk, dh), 1)
    minus_lse = jnp.where(chunk_lane < 3, -1.0, 0.0).astype(jnp.bfloat16)
    minus_delta = jnp.where((chunk_lane >= 3) & (chunk_lane < 6), -1.0, 0.0).astype(jnp.bfloat16)
    key_iota = lax.broadcasted_iota(jnp.int32, (chunk, n_rows), 0)
    my_block = chip * chunk // BLOCK
    far = chips * chunk

    def grads(k, its_chip, diagonal):
        keys = jnp.concatenate([kv[k, 0, 0], kv[k, 1, 0]], axis=0)
        values = jnp.concatenate([kv[k, 0, 1], kv[k, 1, 1]], axis=0)
        keys_more = jnp.concatenate([keys, minus_lse], axis=1)
        values_more = jnp.concatenate([values, minus_delta], axis=1)
        seen = vis_ref[my_block, its_chip * chunk // BLOCK]
        key_pos = key_iota + its_chip * chunk
        key_grad = value_grad = None
        for e in range(CORES):
            q, more, g = rows[e, 0], rows[e, 1], rows[e, 2]
            scores = dot(keys_more, jnp.concatenate([q, more], axis=1), NT)
            grad_prob = dot(values_more, jnp.concatenate([g, more], axis=1), NT)
            allowed = key_pos >= jnp.where(seen > 0, starts[e], far)
            if diagonal:
                allowed = allowed & (key_pos <= spots[e])
            prob = jnp.where(allowed, jnp.exp(scores * scale), 0.0)
            grad_score = (prob * grad_prob * scale).astype(jnp.bfloat16)
            v_part = dot(prob.astype(jnp.bfloat16), g, NN)
            k_part = dot(grad_score, q, NN)
            ds_all[k, :, e * n_rows : (e + 1) * n_rows] = grad_score
            key_grad = k_part if key_grad is None else key_grad + k_part
            value_grad = v_part if value_grad is None else value_grad + v_part
        for e in range(CORES):
            part[k, e, 0] = key_grad[e * tok : (e + 1) * tok].astype(jnp.bfloat16)
            part[k, e, 1] = value_grad[e * tok : (e + 1) * tok].astype(jnp.bfloat16)
        return key_grad, value_grad

    def part_copy(k, its_chip, its_core):
        return pltpu.make_async_remote_copy(
            src_ref=part.at[k, its_core],
            dst_ref=back.at[k, core],
            send_sem=part_send.at[k, its_core],
            recv_sem=part_recv.at[k, core],
            device_id=at(its_chip, its_core),
            device_id_type=MESH,
        )

    def part_arrived(k, its_chip, its_core):
        pltpu.make_async_remote_copy(
            src_ref=part.at[k, its_core],
            dst_ref=back.at[k, its_core],
            send_sem=part_send.at[k, its_core],
            recv_sem=part_recv.at[k, its_core],
            device_id=at(its_chip, its_core),
            device_id_type=MESH,
        ).wait_recv()

    kv_arrived(0, chip, other)
    x_copy.wait_recv()
    grads(0, chip, True)
    part_copy(0, chip, other).start()
    back[0, pl.ds(core, 1)] = part[0, pl.ds(core, 1)]

    def one_chunk(k):
        its_chip = chip - k

        @pl.when(its_chip >= 0)
        def _():
            for e in range(CORES):
                kv_arrived(k, its_chip, e)
            grads(k, its_chip, False)
            for e in range(CORES):
                part_copy(k, its_chip, e).start()

        @pl.when(its_chip < 0)
        def _():
            kv[k] = jnp.zeros(kv.shape[1:], kv.dtype)
            ds_all[k] = jnp.zeros(ds_all.shape[1:], ds_all.dtype)

    each(1, reach + 1, one_chunk, True)

    total = reach + 1
    at_once = max(n for n in range(1, 9) if total % n == 0)

    def query_part(first):
        scores = jnp.concatenate([ds_all[first + i] for i in range(at_once)], axis=0)
        keys = jnp.concatenate(
            [kv[first + i, e, 0] for i in range(at_once) for e in range(CORES)], axis=0
        )
        return dot(scores, keys, TN)

    if total == at_once:
        query_grad = query_part(0)
    else:
        query_grad = lax.fori_loop(
            0, total // at_once, lambda i, acc: acc + query_part(i * at_once),
            jnp.zeros((CORES * n_rows, dh), jnp.float32),
        )
    for e in range(CORES):
        dq_out[e] = query_grad[e * n_rows : (e + 1) * n_rows].astype(jnp.bfloat16)
    dq_copy = pltpu.make_async_remote_copy(
        src_ref=dq_out.at[other],
        dst_ref=dq_back,
        send_sem=dq_send,
        recv_sem=dq_recv,
        device_id=at(chip, other),
        device_id_type=MESH,
    )
    dq_copy.start()
    for h in range(group):
        r = slice(h * tok, (h + 1) * tok)
        dq_ref[:, pl.ds(pl.multiple_of((core * group + h) * dh, dh), dh)] = dq_out[core, r]
    dq_copy.wait_recv()
    for h in range(group):
        r = slice(h * tok, (h + 1) * tok)
        dq_ref[:, pl.ds(pl.multiple_of((other * group + h) * dh, dh), dh)] = dq_back[r]

    part_arrived(0, chip, other)
    for c in range(CORES):
        for which in range(2):
            own_part[c, which] = back[0, c, which].astype(jnp.float32)

    def add(k, its_chip):
        for c in range(CORES):
            part_arrived(k, its_chip, c)
            own_part[c] += back[k, c].astype(jnp.float32)

    on_chips(1, reach + 1, 1, add)
    for c in range(CORES):
        dk_ref[:, c * dh : (c + 1) * dh] = own_part[c, 0].astype(jnp.bfloat16)
        dv_ref[:, c * dh : (c + 1) * dh] = own_part[c, 1].astype(jnp.bfloat16)

    x_copy.wait_send()
    dq_copy.wait_send()
    kv_copy(0, chip, other).wait_send()
    part_copy(0, chip, other).wait_send()

    def kv_left(k, its_chip):
        for c in range(CORES):
            kv_copy(k, its_chip, c).wait_send()

    def part_left(k, its_chip):
        for c in range(CORES):
            part_copy(k, its_chip, c).wait_send()

    on_chips(1, reach + 1, 1, kv_left)
    on_chips(1, reach + 1, -1, part_left)


def store(a_in, b_in, c_in, a_out, b_out, c_out, sem):
    copies = [
        pltpu.make_async_copy(src, dst, sem.at[i])
        for i, (src, dst) in enumerate(((a_in, a_out), (b_in, b_out), (c_in, c_out)))
    ]
    for copy in copies:
        copy.start()
    for copy in copies:
        copy.wait()


def solution(mesh):
    blk_size = mesh.shape["blk"]
    devices = mesh.shape["head"] * blk_size
    chips = devices // CORES

    def shards(queries, key_rows, value_rows, fwd_output, grad_out, log_norm, visible, seg_lengths):
        tok, width = queries.shape
        heads = log_norm.shape[1]
        dh = width // heads
        kv_heads = key_rows.shape[1] // dh
        assert kv_heads == CORES and blk_size % CORES == 0 and BLOCK % (CORES * tok) == 0
        group = heads // kv_heads
        longest = devices * tok // 2
        reach = min(pl.cdiv(longest - 1, CORES * tok), chips - 1)
        n_rows = group * tok
        bf16, f32 = jnp.bfloat16, jnp.float32
        slots = reach + 1
        dma = pltpu.SemaphoreType.DMA
        grads = pl.pallas_call(
            functools.partial(kernel, chips, reach, blk_size, group),
            out_shape=(
                jax.ShapeDtypeStruct(queries.shape, bf16),
                jax.ShapeDtypeStruct(key_rows.shape, bf16),
                jax.ShapeDtypeStruct(value_rows.shape, bf16),
            ),
            in_specs=[pl.BlockSpec(memory_space=pltpu.HBM)] * 8,
            out_specs=[pl.BlockSpec(memory_space=pltpu.VMEM)] * 3,
            scratch_shapes=[
                pltpu.SMEM(visible.shape, jnp.int32),
                pltpu.SMEM(seg_lengths.shape, jnp.int32),
                pltpu.VMEM(queries.shape, bf16),
                pltpu.VMEM(key_rows.shape, bf16),
                pltpu.VMEM(value_rows.shape, bf16),
                pltpu.VMEM(fwd_output.shape, bf16),
                pltpu.VMEM(grad_out.shape, bf16),
                pltpu.VMEM(log_norm.shape[::-1], f32),
                dma((8,)),
                pltpu.VMEM((CORES, 3, n_rows, dh), bf16),
                pltpu.VMEM((3, n_rows, dh), bf16),
                pltpu.VMEM((CORES, 2, tok, dh), bf16),
                pltpu.VMEM((slots, CORES, 2, tok, dh), bf16),
                pltpu.VMEM((slots, CORES * tok, CORES * n_rows), bf16),
                pltpu.VMEM((slots, CORES, 2, tok, dh), bf16),
                pltpu.VMEM((slots, CORES, 2, tok, dh), bf16),
                pltpu.VMEM((CORES, 2, tok, dh), f32),
                pltpu.VMEM((CORES, n_rows, dh), bf16),
                pltpu.VMEM((n_rows, dh), bf16),
                dma, dma,
                dma((slots, CORES)), dma((slots, CORES)),
                dma((slots, CORES)), dma((slots, CORES)),
                dma, dma,
            ],
            compiler_params=pltpu.CompilerParams(
                collective_id=0, has_side_effects=True, vmem_limit_bytes=48 << 20
            ),
        )(
            *(
                pltpu.with_memory_space_constraint(x, pltpu.HBM)
                for x in (visible, seg_lengths, queries, key_rows, value_rows, fwd_output, grad_out, log_norm.T)
            ),
        )

        return pl.pallas_call(
            store,
            out_shape=[jax.ShapeDtypeStruct(g.shape, g.dtype) for g in grads],
            in_specs=[pl.BlockSpec(memory_space=pltpu.VMEM)] * 3,
            out_specs=[pl.BlockSpec(memory_space=pltpu.HBM)] * 3,
            scratch_shapes=[dma((3,))],
            compiler_params=pltpu.CompilerParams(vmem_limit_bytes=1 << 20),
        )(*grads)

    tokens = P(("groups", "head", "blk"), None)
    return jax.shard_map(
        shards,
        mesh=mesh,
        in_specs=(tokens,) * 6 + (P("groups", None), P("groups")),
        out_specs=(tokens,) * 3,
        check_vma=False,
    )
```

```python
import functools
import math

import jax
import jax.numpy as jnp
from jax import lax
from jax.experimental import pallas as pl
from jax.experimental.pallas import tpu as pltpu
from jax.sharding import PartitionSpec as P

BLOCK = 128
CORES = 2
MESH = pl.DeviceIdType.MESH
NT = (((1,), (1,)), ((), ()))
TN = (((0,), (0,)), ((), ()))
NN = (((1,), (0,)), ((), ()))


def dot(a, b, dims):
    return lax.dot_general(a, b, dims, preferred_element_type=jnp.float32)


def each(first, last, body, down=False):
    if last - first <= 8:
        for k in range(last - 1, first - 1, -1) if down else range(first, last):
            body(k)
    else:
        lax.fori_loop(first, last, lambda k, c: (body(k), c)[1], 0)


def kernel(
    chips, reach, blk_size, group,
    vis_hbm, seg_hbm, q_hbm, k_hbm, v_hbm, o_hbm, g_hbm, l_hbm,
    dq_ref, dk_ref, dv_ref,
    vis_ref, seg_ref, q_in, k_in, v_in, o_in, g_in, l_in, in_sem,
    rows, rows_out, kv_out, kv, ds_all, part, back, own_part, dq_out, dq_back,
    x_send, x_recv, kv_send, kv_recv, part_send, part_recv, dq_send, dq_recv,
):
    tok, width = q_in.shape
    dh = k_in.shape[1] // CORES
    half = group * dh
    scale = 1.0 / math.sqrt(dh)
    spot = lax.axis_index("head") * blk_size + lax.axis_index("blk")
    chip, core = spot // CORES, spot % CORES
    other = 1 - core

    def at(its_chip, its_core):
        if blk_size == CORES:
            return {"head": its_chip, "blk": its_core}
        per_head = blk_size // CORES
        return {"head": its_chip // per_head, "blk": its_chip % per_head * CORES + its_core}

    def on_chips(first, last, sign, body, down=False):
        def one(k):
            its_chip = chip + sign * k

            @pl.when((its_chip >= 0) & (its_chip < chips))
            def _():
                body(k, its_chip)

        each(first, last, one, down)

    barrier = pltpu.get_barrier_semaphore()

    def greet(k, its_chip):
        for c in range(CORES):
            pl.semaphore_signal(barrier, inc=1, device_id=at(its_chip, c), device_id_type=MESH)

    loads = [
        pltpu.make_async_copy(src, dst, in_sem.at[i])
        for i, (src, dst) in enumerate(
            ((k_hbm, k_in), (v_hbm, v_in), (q_hbm, q_in), (g_hbm, g_in), (o_hbm, o_in), (l_hbm, l_in),
             (vis_hbm, vis_ref), (seg_hbm, seg_ref))
        )
    ]
    on_chips(1, reach + 1, -1, greet, True)
    on_chips(1, reach + 1, 1, greet, True)
    pl.semaphore_signal(barrier, inc=1, device_id=at(chip, other), device_id_type=MESH)
    for load in loads:
        load.start()

    loads[0].wait()
    loads[1].wait()
    for c in range(CORES):
        kv_out[c, 0] = k_in[:, c * dh : (c + 1) * dh]
        kv_out[c, 1] = v_in[:, c * dh : (c + 1) * dh]
    kv[0, pl.ds(core, 1)] = kv_out[pl.ds(core, 1)]

    near = jnp.minimum(chip, reach) + jnp.minimum(chips - 1 - chip, reach)
    pl.semaphore_wait(barrier, CORES * near + 1)

    def kv_copy(k, its_chip, its_core):
        return pltpu.make_async_remote_copy(
            src_ref=kv_out.at[its_core],
            dst_ref=kv.at[k, core],
            send_sem=kv_send.at[k, its_core],
            recv_sem=kv_recv.at[k, core],
            device_id=at(its_chip, its_core),
            device_id_type=MESH,
        )

    def kv_arrived(k, its_chip, its_core):
        pltpu.make_async_remote_copy(
            src_ref=kv_out.at[0],
            dst_ref=kv.at[k, its_core],
            send_sem=kv_send.at[k, its_core],
            recv_sem=kv_recv.at[k, its_core],
            device_id=at(its_chip, its_core),
            device_id_type=MESH,
        ).wait_recv()

    def send_kv(k, its_chip):
        for c in range(CORES):
            kv_copy(k, its_chip, c).start()

    on_chips(1, reach + 1, 1, send_kv, True)
    kv_copy(0, chip, other).start()

    for load in loads[2:]:
        load.wait()

    lane = lax.broadcasted_iota(jnp.int32, (tok, dh), 1)

    lse_in = jnp.transpose(l_in[...])

    def prepare(column):
        at_h = pl.ds(pl.multiple_of(column * dh, dh), dh)
        g_h = g_in[:, at_h]
        delta = jnp.sum(g_h.astype(jnp.float32) * o_in[:, at_h].astype(jnp.float32), axis=1, keepdims=True)
        return at_h, g_h, delta

    def extra(lse, delta):
        value = jnp.where(lane < 3, lse * (1.0 / scale), jnp.where(lane < 6, delta, 0.0))
        high = value.astype(jnp.bfloat16).astype(jnp.float32)
        rest = value - high
        middle = rest.astype(jnp.bfloat16).astype(jnp.float32)
        third = (lane == 0) | (lane == 3)
        second = (lane == 1) | (lane == 4)
        return jnp.where(third, high, jnp.where(second, middle, rest - middle)).astype(jnp.bfloat16)

    def fill(target, mine):
        base = mine * group
        lse_all = jnp.where(mine == 0, lse_in[:, :group], lse_in[:, group:])
        for h in range(group):
            at_h, g_h, delta = prepare(base + h)
            r = slice(h * tok, (h + 1) * tok)
            target[0, r] = q_in[:, at_h]
            target[1, r] = extra(lse_all[:, h : h + 1], delta)
            target[2, r] = g_h

    fill(rows_out, other)
    x_copy = pltpu.make_async_remote_copy(
        src_ref=rows_out,
        dst_ref=rows.at[core],
        send_sem=x_send,
        recv_sem=x_recv,
        device_id=at(chip, other),
        device_id_type=MESH,
    )
    x_copy.start()
    fill(rows.at[core], core)

    n_rows = group * tok
    row_iota = lax.broadcasted_iota(jnp.int32, (1, n_rows), 1) % tok
    starts, spots = [], []
    for e in range(CORES):
        query_pos = (chip * CORES + e) * tok + row_iota
        start = jnp.zeros_like(query_pos)
        end = jnp.int32(0)
        for s in range(seg_ref.shape[0]):
            end = end + seg_ref[s]
            start = jnp.where(query_pos >= end, end, start)
        starts.append(start)
        spots.append(query_pos)
    chunk = CORES * tok
    chunk_lane = lax.broadcasted_iota(jnp.int32, (chunk, dh), 1)
    minus_lse = jnp.where(chunk_lane < 3, -1.0, 0.0).astype(jnp.bfloat16)
    minus_delta = jnp.where((chunk_lane >= 3) & (chunk_lane < 6), -1.0, 0.0).astype(jnp.bfloat16)
    key_iota = lax.broadcasted_iota(jnp.int32, (chunk, n_rows), 0)
    my_block = chip * chunk // BLOCK
    far = chips * chunk

    def grads(k, its_chip, diagonal):
        keys = jnp.concatenate([kv[k, 0, 0], kv[k, 1, 0]], axis=0)
        values = jnp.concatenate([kv[k, 0, 1], kv[k, 1, 1]], axis=0)
        keys_more = jnp.concatenate([keys, minus_lse], axis=1)
        values_more = jnp.concatenate([values, minus_delta], axis=1)
        seen = vis_ref[my_block, its_chip * chunk // BLOCK]
        key_pos = key_iota + its_chip * chunk
        key_grad = value_grad = None
        for e in range(CORES):
            q, more, g = rows[e, 0], rows[e, 1], rows[e, 2]
            scores = dot(keys_more, jnp.concatenate([q, more], axis=1), NT)
            grad_prob = dot(values_more, jnp.concatenate([g, more], axis=1), NT)
            allowed = key_pos >= jnp.where(seen > 0, starts[e], far)
            if diagonal:
                allowed = allowed & (key_pos <= spots[e])
            prob = jnp.where(allowed, jnp.exp(scores * scale), 0.0)
            grad_score = (prob * grad_prob * scale).astype(jnp.bfloat16)
            v_part = dot(prob.astype(jnp.bfloat16), g, NN)
            k_part = dot(grad_score, q, NN)
            ds_all[k, :, e * n_rows : (e + 1) * n_rows] = grad_score
            key_grad = k_part if key_grad is None else key_grad + k_part
            value_grad = v_part if value_grad is None else value_grad + v_part
        for e in range(CORES):
            part[k, e, 0] = key_grad[e * tok : (e + 1) * tok].astype(jnp.bfloat16)
            part[k, e, 1] = value_grad[e * tok : (e + 1) * tok].astype(jnp.bfloat16)
        return key_grad, value_grad

    def part_copy(k, its_chip, its_core):
        return pltpu.make_async_remote_copy(
            src_ref=part.at[k, its_core],
            dst_ref=back.at[k, core],
            send_sem=part_send.at[k, its_core],
            recv_sem=part_recv.at[k, core],
            device_id=at(its_chip, its_core),
            device_id_type=MESH,
        )

    def part_arrived(k, its_chip, its_core):
        pltpu.make_async_remote_copy(
            src_ref=part.at[k, its_core],
            dst_ref=back.at[k, its_core],
            send_sem=part_send.at[k, its_core],
            recv_sem=part_recv.at[k, its_core],
            device_id=at(its_chip, its_core),
            device_id_type=MESH,
        ).wait_recv()

    x_copy.wait_recv()
    def one_chunk(k):
        its_chip = chip - k

        @pl.when(its_chip >= 0)
        def _():
            for e in range(CORES):
                kv_arrived(k, its_chip, e)
            grads(k, its_chip, False)
            for e in range(CORES):
                part_copy(k, its_chip, e).start()

        @pl.when(its_chip < 0)
        def _():
            kv[k] = jnp.zeros(kv.shape[1:], kv.dtype)
            ds_all[k] = jnp.zeros(ds_all.shape[1:], ds_all.dtype)

    each(1, reach + 1, one_chunk, True)
    kv_arrived(0, chip, other)
    grads(0, chip, True)
    part_copy(0, chip, other).start()
    back[0, pl.ds(core, 1)] = part[0, pl.ds(core, 1)]


    total = reach + 1
    at_once = max(n for n in range(1, 9) if total % n == 0)

    def query_part(first, e):
        mine = pl.ds(pl.multiple_of(e * n_rows, n_rows), n_rows)
        scores = jnp.concatenate([ds_all[first + i, :, mine] for i in range(at_once)], axis=0)
        keys = jnp.concatenate(
            [kv[first + i, c, 0] for i in range(at_once) for c in range(CORES)], axis=0
        )
        return dot(scores, keys, TN)

    def query_grad(e):
        if total == at_once:
            grad = query_part(0, e)
        else:
            grad = lax.fori_loop(
                0, total // at_once, lambda i, acc: acc + query_part(i * at_once, e),
                jnp.zeros((n_rows, dh), jnp.float32),
            )
        dq_out[e] = grad.astype(jnp.bfloat16)

    query_grad(other)
    dq_copy = pltpu.make_async_remote_copy(
        src_ref=dq_out.at[other],
        dst_ref=dq_back,
        send_sem=dq_send,
        recv_sem=dq_recv,
        device_id=at(chip, other),
        device_id_type=MESH,
    )
    dq_copy.start()
    query_grad(core)
    for h in range(group):
        r = slice(h * tok, (h + 1) * tok)
        dq_ref[:, pl.ds(pl.multiple_of((core * group + h) * dh, dh), dh)] = dq_out[core, r]
    dq_copy.wait_recv()
    for h in range(group):
        r = slice(h * tok, (h + 1) * tok)
        dq_ref[:, pl.ds(pl.multiple_of((other * group + h) * dh, dh), dh)] = dq_back[r]

    part_arrived(0, chip, other)
    for c in range(CORES):
        for which in range(2):
            own_part[c, which] = back[0, c, which].astype(jnp.float32)

    def add(k, its_chip):
        for c in range(CORES):
            part_arrived(k, its_chip, c)
            own_part[c] += back[k, c].astype(jnp.float32)

    on_chips(1, reach + 1, 1, add)
    for c in range(CORES):
        dk_ref[:, c * dh : (c + 1) * dh] = own_part[c, 0].astype(jnp.bfloat16)
        dv_ref[:, c * dh : (c + 1) * dh] = own_part[c, 1].astype(jnp.bfloat16)

    x_copy.wait_send()
    dq_copy.wait_send()
    kv_copy(0, chip, other).wait_send()
    part_copy(0, chip, other).wait_send()

    def kv_left(k, its_chip):
        for c in range(CORES):
            kv_copy(k, its_chip, c).wait_send()

    def part_left(k, its_chip):
        for c in range(CORES):
            part_copy(k, its_chip, c).wait_send()

    on_chips(1, reach + 1, 1, kv_left)
    on_chips(1, reach + 1, -1, part_left)


def store(a_in, b_in, c_in, a_out, b_out, c_out, sem):
    copies = [
        pltpu.make_async_copy(src, dst, sem.at[i])
        for i, (src, dst) in enumerate(((a_in, a_out), (b_in, b_out), (c_in, c_out)))
    ]
    for copy in copies:
        copy.start()
    for copy in copies:
        copy.wait()


def solution(mesh):
    blk_size = mesh.shape["blk"]
    devices = mesh.shape["head"] * blk_size
    chips = devices // CORES

    def shards(queries, key_rows, value_rows, fwd_output, grad_out, log_norm, visible, seg_lengths):
        tok, width = queries.shape
        heads = log_norm.shape[1]
        dh = width // heads
        kv_heads = key_rows.shape[1] // dh
        assert kv_heads == CORES and blk_size % CORES == 0 and BLOCK % (CORES * tok) == 0
        group = heads // kv_heads
        longest = devices * tok // 2
        reach = min(pl.cdiv(longest - 1, CORES * tok), chips - 1)
        n_rows = group * tok
        bf16, f32 = jnp.bfloat16, jnp.float32
        slots = reach + 1
        dma = pltpu.SemaphoreType.DMA
        grads = pl.pallas_call(
            functools.partial(kernel, chips, reach, blk_size, group),
            out_shape=(
                jax.ShapeDtypeStruct(queries.shape, bf16),
                jax.ShapeDtypeStruct(key_rows.shape, bf16),
                jax.ShapeDtypeStruct(value_rows.shape, bf16),
            ),
            in_specs=[pl.BlockSpec(memory_space=pltpu.HBM)] * 8,
            out_specs=[pl.BlockSpec(memory_space=pltpu.VMEM)] * 3,
            scratch_shapes=[
                pltpu.SMEM(visible.shape, jnp.int32),
                pltpu.SMEM(seg_lengths.shape, jnp.int32),
                pltpu.VMEM(queries.shape, bf16),
                pltpu.VMEM(key_rows.shape, bf16),
                pltpu.VMEM(value_rows.shape, bf16),
                pltpu.VMEM(fwd_output.shape, bf16),
                pltpu.VMEM(grad_out.shape, bf16),
                pltpu.VMEM(log_norm.shape[::-1], f32),
                dma((8,)),
                pltpu.VMEM((CORES, 3, n_rows, dh), bf16),
                pltpu.VMEM((3, n_rows, dh), bf16),
                pltpu.VMEM((CORES, 2, tok, dh), bf16),
                pltpu.VMEM((slots, CORES, 2, tok, dh), bf16),
                pltpu.VMEM((slots, CORES * tok, CORES * n_rows), bf16),
                pltpu.VMEM((slots, CORES, 2, tok, dh), bf16),
                pltpu.VMEM((slots, CORES, 2, tok, dh), bf16),
                pltpu.VMEM((CORES, 2, tok, dh), f32),
                pltpu.VMEM((CORES, n_rows, dh), bf16),
                pltpu.VMEM((n_rows, dh), bf16),
                dma, dma,
                dma((slots, CORES)), dma((slots, CORES)),
                dma((slots, CORES)), dma((slots, CORES)),
                dma, dma,
            ],
            compiler_params=pltpu.CompilerParams(
                collective_id=0, has_side_effects=True, vmem_limit_bytes=48 << 20
            ),
        )(
            *(
                pltpu.with_memory_space_constraint(x, pltpu.HBM)
                for x in (visible, seg_lengths, queries, key_rows, value_rows, fwd_output, grad_out, log_norm.T)
            ),
        )

        return pl.pallas_call(
            store,
            out_shape=[jax.ShapeDtypeStruct(g.shape, g.dtype) for g in grads],
            in_specs=[pl.BlockSpec(memory_space=pltpu.VMEM)] * 3,
            out_specs=[pl.BlockSpec(memory_space=pltpu.HBM)] * 3,
            scratch_shapes=[dma((3,))],
            compiler_params=pltpu.CompilerParams(vmem_limit_bytes=1 << 20),
        )(*grads)

    tokens = P(("groups", "head", "blk"), None)
    return jax.shard_map(
        shards,
        mesh=mesh,
        in_specs=(tokens,) * 6 + (P("groups", None), P("groups")),
        out_specs=(tokens,) * 3,
        check_vma=False,
    )
```
